32 devices in a mesh: patch: 8 (over z, core), visit: 4 (over y, x).
Axes of the slice: x: 2, y: 2, z: 4, core: 2. Of those that a mesh axis runs over, the one named last changes fastest.
Arguments:
- blocks: bfloat16 [8, 4, 16, 256, 256], P('patch', 'visit'), may hold values from -6 to 6
- block_patch: int32 [8, 4, 16, 1], P('patch', 'visit'), may hold values from 0 to 7; in each aligned block of 16 rows (0 to 15, 16 to 31, ..., all dimensions but the last counted through in order) at most 2 rows name the same one
- block_slot: int32 [8, 4, 16], P('patch', 'visit'), may hold values from 0 to 7
- block_count: int32 [8, 4], P('patch', 'visit'), may hold values from 12 to 16, as said below
- template: bfloat16 [8, 512, 1024], P('patch', 'visit'), may hold values from -6 to 6
- basis_rows: bfloat16 [9, 21], replicated, may hold values from -1.25 to 1.25
- basis_cols: float32 [9, 21], replicated, may hold values from -1.25 to 1.25
- coeffs: float32 [4, 9], P('visit'), may hold values from -2 to 2
- psf_rows: bfloat16 [4, 2, 25], P('visit'), may hold values from -1.25 to 1.25
- psf_cols: bfloat16 [4, 2, 25], P('visit'), may hold values from -1.25 to 1.25
Outputs:
- filtered: float32 [8, 4, 512, 1024], P('patch', 'visit')
The draws below stay inside these ranges and needn't reach their ends.
Inputs may be any that keep to these rules, and one draw needn't show every extreme that they name: `block_patch`: among the 16 entries of one list (one patch index and visit) no patch is named more than 2 times, and some list names a patch exactly 2 times. Entries at positions block_count and beyond are unused.
All inputs are finite; a program needn't handle non-finite values.
Results may differ from the reference program's by a relative error of at most 0.005.
Values may be sent and summed in bfloat16 or wider, within the bound.
A program may use at most 128 MiB of HBM per device.

```python
import math
import jax
import jax.numpy as jnp
import numpy as np
from jax import lax

BLK = 256
PATCH_ROWS = 512
PATCH_COLS = 1024
NB_DEV = 16
CAP = 2
NBASIS = 9
KBASIS = 21
KPSF = 25
NPSF = 2
SLOTS = 8
N_PATCH = 8
N_VISIT = 4


def draw_block_count(key, part):
    counts = jax.random.randint(key, (N_PATCH, N_VISIT), 3 * NB_DEV // 4, NB_DEV + 1)
    counts = counts.at[0, 0].set(NB_DEV)
    counts = counts.at[N_PATCH - 1, N_VISIT - 1].set(3 * NB_DEV // 4)
    return counts.astype(jnp.int32)


def plant(array, rng, smallest, high):
    index_at = [jax.random.randint(jax.random.fold_in(rng, axis), (), 0, length) for axis, length in enumerate(array.shape)]
    longest = array.shape.index(max(array.shape))
    beside = index_at[:longest] + [(index_at[longest] + 1) % array.shape[longest]] + index_at[longest + 1:]
    return array.at[tuple(index_at)].set(smallest).at[tuple(beside)].set(high)


def steps_of(rng, dims, split, least, high):
    factor_of = 1.0
    for position, blocks in split:
        draws = jax.random.uniform(jax.random.fold_in(jax.random.fold_in(rng, 6), position), (blocks,), jnp.float32, least / len(split), high / len(split))
        factor_of = factor_of * jnp.repeat(jnp.exp(draws), dims[position] // blocks).reshape((-1,) + (1,) * (len(dims) - 1 - position))
    return factor_of


def assign_block(own_key, own, number, rows, amount, top, limit, lean):
    order = jax.random.permutation(own_key, amount)
    crowded, ordinary = shares(amount, rows * top, limit, lean, True), shares(amount, rows * top, limit, lean, False)
    places = jnp.arange(amount)

    def named(sizes, offset_by):
        used = int((sizes > 0).sum())
        fixed = max(1, used // 4)
        shifted = fixed + (places - fixed + offset_by * (used - fixed)) % max(1, amount - fixed)
        return jnp.zeros((amount,), jnp.int32).at[order[jnp.where(places < fixed, places, shifted)]].set(jnp.asarray(sizes, jnp.int32))

    sizes = jnp.where(number % 4 == 0, named(crowded, number // 4), named(ordinary, number - number // 4 - 1))
    mixed = jax.random.permutation(jax.random.fold_in(own, 3), amount)
    giver, taker = mixed[0:amount // 2 * 2:2], mixed[1:amount // 2 * 2:2]
    slack = jnp.minimum(sizes[giver] - 1, limit - sizes[taker]) // 2
    slack = jnp.where((giver == order[0]) | (taker == order[0]) | (sizes[taker] == 0), 0, jnp.maximum(slack, 0))
    shifted = jax.random.randint(jax.random.fold_in(own, 4), (amount // 2,), 0, 1 << 20) % (slack + 1)
    sizes = sizes.at[giver].add(-shifted).at[taker].add(shifted)
    labels = jnp.searchsorted(jnp.cumsum(sizes), jnp.arange(rows * top), side="right").astype(jnp.int32)
    listing = labels.reshape(top, rows).T
    listing = listing[jax.random.permutation(jax.random.fold_in(own, 1), rows)]
    offset_by = jax.random.randint(jax.random.fold_in(own, 2), (rows, 1), 0, top)
    return jnp.take_along_axis(listing, (jnp.arange(top)[None, :] + offset_by) % top, axis=1)


def shares(count, total, bound, skew, full):
    loads = [(1 << 20) // math.isqrt(grade ** skew) + 1 for grade in range(1, count + 1)]
    largest = bound if full else min(bound, max(-(-total // count), total * loads[0] // sum(loads)))
    least = 1 if total - largest >= count - 1 else 0
    given, rest = [largest] + [least] * (count - 1), total - largest - least * (count - 1)
    while rest > 0:
        free = [i for i in range(1, count) if given[i] < largest] or [i for i in range(1, count) if given[i] < bound]
        mass, remaining = sum([loads[i] for i in free]), rest
        for i in free:
            addition = min(bound - given[i], max(1, remaining * loads[i] // mass), rest)
            given[i] = given[i] + addition
            rest = rest - addition
    return np.array(given)


def noise(rng, shape, scale, most, shards=(), held_as=jnp.bfloat16):
    values = scale * jax.random.normal(rng, shape, jnp.float32)
    if shards:
        values = values * steps_of(rng, shape, shards, -0.22, 0.18)
    return jnp.clip(values, -most, most).astype(held_as)


def setup_inputs(seed: int = 0) -> dict:
    seeds = jax.random.split(jax.random.key(seed), 11)
    blocks = noise(seeds[0], (N_PATCH, N_VISIT, NB_DEV, BLK, BLK), 1.0, 6.0, ((0, 8), (1, 4)))
    block_patch_keys = jax.random.split(jax.random.fold_in(seeds[1], 1), N_PATCH * N_VISIT * NB_DEV // NB_DEV)
    block_patch_turns = jax.random.permutation(jax.random.fold_in(seeds[1], 3), N_PATCH * N_VISIT * NB_DEV // NB_DEV)
    block_patch = jax.vmap(lambda own, number: assign_block(jax.random.fold_in(seeds[1], 2), own, number, NB_DEV, N_PATCH, 1, CAP, 2))(block_patch_keys, block_patch_turns).reshape((N_PATCH, N_VISIT, NB_DEV, 1))
    block_slot = plant(jax.random.randint(seeds[2], (N_PATCH, N_VISIT, NB_DEV), 0, SLOTS), jax.random.fold_in(seeds[2], 1), 0, SLOTS - 1).astype(jnp.int32)
    block_count = draw_block_count(jax.random.fold_in(seeds[10], 71), 0)
    template = noise(seeds[4], (N_PATCH, PATCH_ROWS, PATCH_COLS), 1.0, 6.0, ((0, 8), (1, 4)))
    basis_rows = noise(seeds[5], (NBASIS, KBASIS), KBASIS ** -0.5, 1.25)
    basis_cols = noise(seeds[6], (NBASIS, KBASIS), KBASIS ** -0.5, 1.25, (), jnp.float32)
    coeffs = noise(seeds[7], (N_VISIT, NBASIS), 0.33, 2.0, ((0, 4),), jnp.float32)
    psf_rows = noise(seeds[8], (N_VISIT, NPSF, KPSF), KPSF ** -0.5, 1.25, ((0, 4),))
    psf_cols = noise(seeds[9], (N_VISIT, NPSF, KPSF), KPSF ** -0.5, 1.25, ((0, 4),))
    return {"blocks": blocks, "block_patch": block_patch, "block_slot": block_slot, "block_count": block_count, "template": template, "basis_rows": basis_rows, "basis_cols": basis_cols, "coeffs": coeffs, "psf_rows": psf_rows, "psf_cols": psf_cols}


def rounded(values):
    return lax.optimization_barrier(values.astype(jnp.bfloat16)).astype(jnp.float32)


def correlate(source, kernel_taps, along_axis):
    length = kernel_taps.shape[-1]
    half_len = length // 2
    extent = source.shape[along_axis]
    padding = [(0, 0)] * source.ndim
    padding[along_axis] = (half_len, half_len)
    padded = jnp.pad(source, padding)
    summed = jnp.zeros(source.shape, jnp.float32)
    for offset in range(length):
        summed = summed + kernel_taps[:, offset][:, None, None] * lax.slice_in_dim(padded, offset, offset + extent, axis=along_axis)
    return summed


def reference(blocks, block_patch, block_slot, block_count, template, basis_rows, basis_cols, coeffs, psf_rows, psf_cols):
    tall_count = PATCH_ROWS // BLK
    wide_count = PATCH_COLS // BLK
    live_mask = jnp.arange(NB_DEV, dtype=jnp.int32)[None, None, :] < block_count[:, :, None]
    destination = block_patch[..., 0]
    row_taps = basis_rows.astype(jnp.float32)

    def one_patch(patch_id):
        source = jnp.broadcast_to(template[patch_id].astype(jnp.float32)[None], (NBASIS, PATCH_ROWS, PATCH_COLS))
        smoothed = rounded(correlate(source, row_taps, 2))

        def one_visit(visit_id):
            chosen = live_mask[:, visit_id] & (destination[:, visit_id] == patch_id)
            segment_ids = jnp.where(chosen, block_slot[:, visit_id], SLOTS).reshape(-1).astype(jnp.int32)
            pieces = blocks[:, visit_id].astype(jnp.float32).reshape(N_PATCH * NB_DEV, BLK * BLK)
            slot_images = jax.ops.segment_sum(pieces, segment_ids, num_segments=SLOTS)
            science = slot_images.reshape(tall_count, wide_count, BLK, BLK).transpose(0, 2, 1, 3).reshape(PATCH_ROWS, PATCH_COLS)
            scaled = rounded(coeffs[visit_id][:, None] * basis_cols)
            model_image = jnp.sum(correlate(smoothed, scaled, 1), axis=0)
            difference = rounded(science - model_image)
            spread = jnp.broadcast_to(difference[None], (NPSF, PATCH_ROWS, PATCH_COLS))
            blurred = rounded(correlate(spread, psf_rows[visit_id].astype(jnp.float32), 2))
            return jnp.sum(correlate(blurred, psf_cols[visit_id].astype(jnp.float32), 1), axis=0)

        return lax.map(one_visit, jnp.arange(N_VISIT, dtype=jnp.int32))

    return lax.map(one_patch, jnp.arange(N_PATCH, dtype=jnp.int32))
```

```python
import functools

import jax
import jax.numpy as jnp
from jax import lax
from jax.experimental import pallas as pl
from jax.experimental.pallas import tpu as pltpu
from jax.sharding import PartitionSpec as P

CAP = 2
LANE = 128
HALF = 64
WIN = 256
F32 = jnp.float32
BF16 = jnp.bfloat16
VMEM_LIMIT = 56 * 1024 * 1024


def column_table(row, half_len):
    wide = jnp.broadcast_to(row, (WIN, WIN))
    return pltpu.roll(wide, (WIN - HALF - half_len) // 8 * 8, 1, stride=1, stride_axis=0)[:, :LANE].astype(BF16)


def row_table(row, half_len):
    wide = jnp.broadcast_to(row, (LANE, WIN))
    return pltpu.roll(wide, (HALF - half_len) // 8 * 8, 1, stride=1, stride_axis=0).astype(BF16)


def shift_into(load_tile, shifted, height, tiles, step):
    def body(r, carry):
        rows = pl.ds(pl.multiple_of(r * step, step), step)
        lane = lax.broadcasted_iota(jnp.int32, (step, LANE), 1)
        before = jnp.zeros((step, LANE), F32)
        for t in range(tiles):
            rolled = pltpu.roll(load_tile(rows, t), HALF, 1)
            shifted[rows, t * LANE : (t + 1) * LANE] = jnp.where(lane < HALF, before, rolled).astype(BF16)
            before = rolled
        shifted[rows, tiles * LANE :] = jnp.where(lane < HALF, before, 0.0).astype(BF16)
        return carry

    lax.fori_loop(0, height // step, body, 0)


def columns_pass(shifted, tables, smooth, pair, count, height):
    for side in range(2):
        start = pl.multiple_of((2 * pair + side) * LANE, LANE)
        window = shifted[:, pl.ds(start, WIN)]
        for group in range(0, count, 2):
            taken = min(2, count - group)
            got = jnp.dot(
                window, tables[:, group * LANE : (group + taken) * LANE], preferred_element_type=F32
            ).astype(BF16)
            for k in range(taken):
                smooth[group + k, HALF : HALF + height, side * LANE : (side + 1) * LANE] = got[
                    :, k * LANE : (k + 1) * LANE
                ]


def rows_pass(smooth, tables, count, r):
    start = pl.multiple_of(r * LANE, LANE)
    total = jnp.zeros((LANE, WIN), F32)
    for k in range(count):
        total = total + jnp.dot(tables[k], smooth[k, pl.ds(start, WIN), :], preferred_element_type=F32)
    return total


def build_tables(column_rows, row_rows, column_tables, row_tables, count, half_c, half_r):
    for k in range(count):
        column_tables[:, k * LANE : (k + 1) * LANE] = column_table(column_rows[k : k + 1, :], half_c)
        row_tables[k] = row_table(row_rows[k : k + 1, :], half_r)


def clear_edges(smooth, count, height):
    for k in range(count):
        smooth[k, :HALF, :] = jnp.zeros((HALF, smooth.shape[2]), BF16)
        smooth[k, HALF + height :, :] = jnp.zeros((HALF, smooth.shape[2]), BF16)


def pack_kernel(places, patch, slot, count, blocks, out, labels, source, named, sems):
    entries = patch.shape[0]

    def reset(d, carry):
        source[d] = 0
        labels[d] = -1
        named[d] = 0
        return carry

    lax.fori_loop(0, places, reset, 0)
    live = count[0]

    def enter(i, carry):
        target = patch[i]
        earlier = named[target]
        named[target] = earlier + 1
        place = target * CAP + earlier

        @pl.when(i < live)
        def _():
            source[place] = i
            labels[place] = slot[i]

        return carry

    lax.fori_loop(0, entries, enter, 0)
    for d in range(places):
        pltpu.make_async_copy(blocks.at[source[d]], out.at[d], sems.at[d]).start()
    for d in range(places):
        pltpu.make_async_copy(blocks.at[0], out.at[d], sems.at[d]).wait()


def model_kernel(halves, template, column_rows, row_rows, model, shifted, column_tables, row_tables, smooth):
    height, breadth = template.shape
    count = column_rows.shape[0]
    build_tables(column_rows, row_rows, column_tables, row_tables, count, *halves)
    clear_edges(smooth, count, height)
    shift_into(
        lambda rows, t: template[rows, t * LANE : (t + 1) * LANE].astype(F32),
        shifted, height, breadth // LANE, 32,
    )

    def per_pair(pair, carry):
        columns_pass(shifted, column_tables, smooth, pair, count, height)

        def per_row(r, inner):
            rows = pl.ds(pl.multiple_of(r * LANE, LANE), LANE)
            columns = pl.ds(pl.multiple_of(pair * WIN, WIN), WIN)
            model[rows, columns] = rows_pass(smooth, row_tables, count, r)
            return inner

        return lax.fori_loop(0, height // LANE, per_row, carry)

    lax.fori_loop(0, breadth // WIN, per_pair, 0)


def final_kernel(halves, labels, arrived, model, column_rows, row_rows, out, total, shifted, column_tables, row_tables, smooth):
    height, breadth = model.shape
    edge = arrived.shape[1]
    wide = breadth // edge
    places = arrived.shape[0]
    count = column_rows.shape[0]
    build_tables(column_rows, row_rows, column_tables, row_tables, count, *halves)
    clear_edges(smooth, count, height)
    total[...] = jnp.zeros(total.shape, F32)

    def add(j, carry):
        s = labels[j]

        @pl.when(s >= 0)
        def _():
            total[s] = total[s] + arrived[j].astype(F32)

        return carry

    lax.fori_loop(0, places, add, 0)
    step = 32
    per_edge = edge // step

    def body(r, carry):
        rows = pl.ds(pl.multiple_of(r * step, step), step)
        tall = r // per_edge
        inside = pl.ds(pl.multiple_of((r % per_edge) * step, step), step)
        lane = lax.broadcasted_iota(jnp.int32, (step, LANE), 1)
        before = jnp.zeros((step, LANE), F32)
        tiles = breadth // LANE
        for t in range(tiles):
            at = t * LANE % edge
            tile = total[tall * wide + t * LANE // edge, inside, at : at + LANE] - model[rows, t * LANE : (t + 1) * LANE]
            rolled = pltpu.roll(tile, HALF, 1)
            shifted[rows, t * LANE : (t + 1) * LANE] = jnp.where(lane < HALF, before, rolled).astype(BF16)
            before = rolled
        shifted[rows, tiles * LANE :] = jnp.where(lane < HALF, before, 0.0).astype(BF16)
        return carry

    lax.fori_loop(0, height // step, body, 0)

    def per_pair(pair, carry):
        columns_pass(shifted, column_tables, smooth, pair, count, height)

        def per_row(r, inner):
            rows = pl.ds(pl.multiple_of(r * LANE, LANE), LANE)
            columns = pl.ds(pl.multiple_of(pair * WIN, WIN), WIN)
            out[rows, columns] = rows_pass(smooth, row_tables, count, r)
            return inner

        return lax.fori_loop(0, height // LANE, per_row, carry)

    lax.fori_loop(0, breadth // WIN, per_pair, 0)


def padded(taps, flip):
    taps = taps.astype(F32)
    if flip:
        taps = taps[:, ::-1]
    lead = (HALF - taps.shape[1] // 2) % 8
    return jnp.pad(taps, ((0, 0), (lead, WIN - lead - taps.shape[1])))


SMEM = pl.BlockSpec(memory_space=pltpu.SMEM)
VMEM = pl.BlockSpec(memory_space=pltpu.VMEM)
ANY = pl.BlockSpec(memory_space=pl.ANY)


def stencil_scratch(count, height, breadth):
    return [
        pltpu.VMEM((height, breadth + LANE), BF16),
        pltpu.VMEM((WIN, count * LANE), BF16),
        pltpu.VMEM((count, LANE, WIN), BF16),
        pltpu.VMEM((count, height + 2 * HALF, WIN), BF16),
    ]


def per_device(blocks, block_patch, block_slot, block_count, template, basis_rows, basis_cols, coeffs, psf_rows, psf_cols):
    n_patch = lax.axis_size("patch")
    n_visit = lax.axis_size("visit")
    local_rows, breadth = template.shape[1:]
    height = local_rows * n_visit
    entries, edge = blocks.shape[2:4]
    places = n_patch * CAP
    slots = height // edge * (breadth // edge)
    outgoing, labels = pl.pallas_call(
        functools.partial(pack_kernel, places),
        out_shape=(
            jax.ShapeDtypeStruct((places, edge, edge), BF16),
            jax.ShapeDtypeStruct((places,), jnp.int32),
        ),
        in_specs=[SMEM, SMEM, SMEM, ANY],
        out_specs=(ANY, SMEM),
        scratch_shapes=[
            pltpu.SMEM((places,), jnp.int32),
            pltpu.SMEM((places,), jnp.int32),
            pltpu.SemaphoreType.DMA((places,)),
        ],
    )(block_patch.reshape(entries), block_slot.reshape(entries), block_count.reshape(1), blocks[0, 0])
    arrived = lax.all_to_all(outgoing, "patch", split_axis=0, concat_axis=0, tiled=True)
    arrived_labels = lax.all_to_all(labels, "patch", split_axis=0, concat_axis=0, tiled=True)
    scaled = (coeffs[0][:, None] * basis_cols).astype(BF16)
    me = lax.axis_index("visit")
    whole = jnp.zeros((height, breadth), BF16)
    whole = lax.dynamic_update_slice(whole, template[0], (me * local_rows, 0))
    for hop in range(1, n_visit):
        moved = lax.ppermute(template[0], "visit", [(d, (d + hop) % n_visit) for d in range(n_visit)])
        whole = lax.dynamic_update_slice(whole, moved, ((me + n_visit - hop) % n_visit * local_rows, 0))
    params = pltpu.CompilerParams(vmem_limit_bytes=VMEM_LIMIT)
    model = pl.pallas_call(
        functools.partial(model_kernel, (basis_rows.shape[1] // 2, basis_cols.shape[1] // 2)),
        out_shape=jax.ShapeDtypeStruct((height, breadth), F32),
        in_specs=[VMEM] * 3,
        out_specs=VMEM,
        scratch_shapes=stencil_scratch(basis_rows.shape[0], height, breadth),
        compiler_params=params,
        cost_estimate=pl.CostEstimate(flops=20_000_000_000, bytes_accessed=4 * height * breadth, transcendentals=0),
    )(whole, padded(basis_rows, True), padded(scaled, False))
    filtered = pl.pallas_call(
        functools.partial(final_kernel, (psf_rows.shape[2] // 2, psf_cols.shape[2] // 2)),
        out_shape=jax.ShapeDtypeStruct((height, breadth), F32),
        in_specs=[SMEM] + [VMEM] * 4,
        out_specs=VMEM,
        scratch_shapes=[pltpu.VMEM((slots, edge, edge), F32)] + stencil_scratch(psf_rows.shape[1], height, breadth),
        compiler_params=params,
    )(arrived_labels, arrived, model, padded(psf_rows[0], True), padded(psf_cols[0], False))
    return filtered[None, None]


def solution(mesh):
    return jax.shard_map(
        per_device,
        mesh=mesh,
        in_specs=(
            P("patch", "visit", None, None, None),
            P("patch", "visit", None, None),
            P("patch", "visit", None),
            P("patch", "visit"),
            P("patch", "visit", None),
            P(),
            P(),
            P("visit", None),
            P("visit", None, None),
            P("visit", None, None),
        ),
        out_specs=P("patch", "visit", None, None),
        check_vma=False,
    )
```

```python
import functools

import jax
import jax.numpy as jnp
from jax import lax
from jax.experimental import pallas as pl
from jax.experimental.pallas import tpu as pltpu
from jax.sharding import PartitionSpec as P

CAP = 2
LANE = 128
HALF = 64
WIN = 256
F32 = jnp.float32
BF16 = jnp.bfloat16
VMEM_LIMIT = 56 * 1024 * 1024


def column_table(row, half_len):
    wide = jnp.broadcast_to(row, (WIN, WIN))
    return pltpu.roll(wide, (WIN - HALF - half_len) // 8 * 8, 1, stride=1, stride_axis=0)[:, :LANE].astype(BF16)


def row_table(row, half_len):
    wide = jnp.broadcast_to(row, (LANE, WIN))
    return pltpu.roll(wide, (HALF - half_len) // 8 * 8, 1, stride=1, stride_axis=0).astype(BF16)


def shift_into(load_tile, shifted, height, tiles, step):
    def body(r, carry):
        rows = pl.ds(pl.multiple_of(r * step, step), step)
        lane = lax.broadcasted_iota(jnp.int32, (step, LANE), 1)
        before = jnp.zeros((step, LANE), F32)
        for t in range(tiles):
            rolled = pltpu.roll(load_tile(rows, t), HALF, 1)
            shifted[rows, t * LANE : (t + 1) * LANE] = jnp.where(lane < HALF, before, rolled).astype(BF16)
            before = rolled
        shifted[rows, tiles * LANE :] = jnp.where(lane < HALF, before, 0.0).astype(BF16)
        return carry

    lax.fori_loop(0, height // step, body, 0)


def columns_pass(shifted, tables, smooth, pair, count, height):
    for side in range(2):
        start = pl.multiple_of((2 * pair + side) * LANE, LANE)
        window = shifted[:, pl.ds(start, WIN)]
        for group in range(0, count, 2):
            taken = min(2, count - group)
            got = jnp.dot(
                window, tables[:, group * LANE : (group + taken) * LANE], preferred_element_type=F32
            ).astype(BF16)
            for k in range(taken):
                smooth[group + k, HALF : HALF + height, side * LANE : (side + 1) * LANE] = got[
                    :, k * LANE : (k + 1) * LANE
                ]


def rows_pass(smooth, tables, count, r):
    start = pl.multiple_of(r * LANE, LANE)
    total = jnp.zeros((LANE, WIN), F32)
    for k in range(count):
        total = total + jnp.dot(tables[k], smooth[k, pl.ds(start, WIN), :], preferred_element_type=F32)
    return total


def build_tables(column_rows, row_rows, column_tables, row_tables, count, half_c, half_r):
    for k in range(count):
        column_tables[:, k * LANE : (k + 1) * LANE] = column_table(column_rows[k : k + 1, :], half_c)
        row_tables[k] = row_table(row_rows[k : k + 1, :], half_r)


def clear_edges(smooth, count, height):
    for k in range(count):
        smooth[k, :HALF, :] = jnp.zeros((HALF, smooth.shape[2]), BF16)
        smooth[k, HALF + height :, :] = jnp.zeros((HALF, smooth.shape[2]), BF16)


def exchange_kernel(
    n_patch, n_visit, halves,
    patch, slot, live, blocks, template, column_rows, row_rows,
    difference,
    raw, outgoing, arrived, labels_out, labels_in, whole, total, shifted, column_tables, row_tables, smooth,
    load_sem, own_sem, block_send, block_recv, label_send, label_recv, rows_send, rows_recv,
):
    me = lax.axis_index("patch")
    my_visit = lax.axis_index("visit")
    local_rows, breadth = template.shape
    height = local_rows * n_visit
    entries, edge = blocks.shape[:2]
    count = column_rows.shape[0]
    wide = breadth // edge
    turn = 1 - 2 * (me // (n_patch // 2))
    peers = [lax.rem(me + turn * hop + n_patch, n_patch) for hop in range(1, n_patch)]
    visits = [lax.rem(my_visit + hop, n_visit) for hop in range(1, n_visit)]

    load = pltpu.make_async_copy(blocks, raw, load_sem)
    load.start()
    my_rows = pl.ds(pl.multiple_of(my_visit * local_rows, local_rows), local_rows)
    own = pltpu.make_async_copy(template, whole.at[my_rows], own_sem)
    own.start()
    barrier = pltpu.get_barrier_semaphore()
    for peer in peers:
        pl.semaphore_signal(barrier, inc=1, device_id={"patch": peer}, device_id_type=pl.DeviceIdType.MESH)
    for visit in visits:
        pl.semaphore_signal(barrier, inc=1, device_id={"visit": visit}, device_id_type=pl.DeviceIdType.MESH)

    targets = [patch[i] for i in range(entries)]
    place_of = []
    for i in range(entries):
        earlier = jnp.int32(0)
        for before in range(i):
            earlier = earlier + jnp.where(targets[before] == targets[i], 1, 0)
        place_of.append(targets[i] * CAP + earlier)
    marks = [jnp.where(i < live[0], slot[i] + 1, 0) for i in range(entries)]
    load.wait()

    def pack(d, carry):
        source = jnp.int32(0)
        label = jnp.int32(-1)
        for i in range(entries):
            source = source + jnp.where(place_of[i] == d, i, 0)
            label = label + jnp.where(place_of[i] == d, marks[i], 0)
        outgoing[d] = raw[source]
        labels_out[d] = jnp.full((8, LANE), label, jnp.int32)
        return carry

    lax.fori_loop(0, n_patch * CAP, pack, 0)
    pl.semaphore_wait(barrier, n_patch + n_visit - 2)

    row_copies = []
    for hop, visit in enumerate(visits):
        row_copies.append(
            pltpu.make_async_remote_copy(
                src_ref=template, dst_ref=whole.at[my_rows],
                send_sem=rows_send.at[hop], recv_sem=rows_recv.at[my_visit],
                device_id={"visit": visit}, device_id_type=pl.DeviceIdType.MESH,
            )
        )
    copies = []
    for hop, peer in enumerate(peers):
        theirs = pl.ds(peer * CAP, CAP)
        mine = pl.ds(me * CAP, CAP)
        for source, target, send, recv in (
            (labels_out, labels_in, label_send, label_recv),
            (outgoing, arrived, block_send, block_recv),
        ):
            copies.append(
                pltpu.make_async_remote_copy(
                    src_ref=source.at[theirs], dst_ref=target.at[mine],
                    send_sem=send.at[hop], recv_sem=recv.at[me],
                    device_id={"patch": peer}, device_id_type=pl.DeviceIdType.MESH,
                )
            )
    for copy in row_copies:
        copy.start()
    for copy in copies:
        copy.start()

    build_tables(column_rows, row_rows, column_tables, row_tables, count, *halves)
    clear_edges(smooth, count, height)
    own.wait()
    for visit in visits:
        rows = pl.ds(pl.multiple_of(visit * local_rows, local_rows), local_rows)
        pltpu.make_async_copy(whole.at[rows], whole.at[rows], rows_recv.at[visit]).wait()
    shift_into(
        lambda rows, t: whole[rows, t * LANE : (t + 1) * LANE].astype(F32),
        shifted, height, breadth // LANE, 32,
    )

    def per_pair(pair, carry):
        columns_pass(shifted, column_tables, smooth, pair, count, height)

        def per_row(r, inner):
            rows = pl.ds(pl.multiple_of(r * LANE, LANE), LANE)
            columns = pl.ds(pl.multiple_of(pair * WIN, WIN), WIN)
            total[rows, columns] = -rows_pass(smooth, row_tables, count, r)
            return inner

        return lax.fori_loop(0, height // LANE, per_row, carry)

    lax.fori_loop(0, breadth // WIN, per_pair, 0)

    def add_from(held, labels, at):
        step = 16
        marks = [labels[at + c][:1] for c in range(CAP)]
        masks = [[jnp.broadcast_to(jnp.where(mark == s, 1.0, 0.0), (step, LANE)) for mark in marks] for s in range(height // edge * wide)]

        def body(r, carry):
            inside = pl.ds(pl.multiple_of(r * step, step), step)
            for lane in range(0, edge, LANE):
                pieces = [held[at + c, inside, lane : lane + LANE].astype(F32) for c in range(CAP)]
                for s in range(height // edge * wide):
                    rows = pl.ds(pl.multiple_of(s // wide * edge + r * step, step), step)
                    columns = slice(s % wide * edge + lane, s % wide * edge + lane + LANE)
                    value = total[rows, columns]
                    for c in range(CAP):
                        value = value + masks[s][c] * pieces[c]
                    total[rows, columns] = value
            return carry

        lax.fori_loop(0, edge // step, body, 0)

    add_from(outgoing, labels_out, me * CAP)
    for peer in peers:
        theirs = pl.ds(peer * CAP, CAP)
        pltpu.make_async_copy(labels_in.at[theirs], labels_in.at[theirs], label_recv.at[peer]).wait()
        pltpu.make_async_copy(arrived.at[theirs], arrived.at[theirs], block_recv.at[peer]).wait()
        add_from(arrived, labels_in, peer * CAP)
    shift_into(
        lambda rows, t: total[rows, t * LANE : (t + 1) * LANE],
        difference, height, breadth // LANE, 32,
    )
    for copy in row_copies + copies:
        copy.wait_send()


def filter_kernel(halves, difference, column_rows, row_rows, out, column_tables, row_tables, smooth):
    height = difference.shape[0]
    count = column_rows.shape[0]
    pair = pl.program_id(0)

    @pl.when(pair == 0)
    def _():
        build_tables(column_rows, row_rows, column_tables, row_tables, count, *halves)
        clear_edges(smooth, count, height)

    columns_pass(difference, column_tables, smooth, pair, count, height)
    for r in range(height // LANE):
        out[r * LANE : (r + 1) * LANE, :] = rows_pass(smooth, row_tables, count, r)


def padded(taps, flip):
    taps = taps.astype(F32)
    if flip:
        taps = taps[:, ::-1]
    lead = (HALF - taps.shape[1] // 2) % 8
    return jnp.pad(taps, ((0, 0), (lead, WIN - lead - taps.shape[1])))


SMEM = pl.BlockSpec(memory_space=pltpu.SMEM)
VMEM = pl.BlockSpec(memory_space=pltpu.VMEM)
ANY = pl.BlockSpec(memory_space=pl.ANY)


def stencil_scratch(count, height, breadth):
    return [
        pltpu.VMEM((height, breadth + LANE), BF16),
        pltpu.VMEM((WIN, count * LANE), BF16),
        pltpu.VMEM((count, LANE, WIN), BF16),
        pltpu.VMEM((count, height + 2 * HALF, WIN), BF16),
    ]


def per_device(blocks, block_patch, block_slot, block_count, template, basis_rows, basis_cols, coeffs, psf_rows, psf_cols):
    n_patch = lax.axis_size("patch")
    n_visit = lax.axis_size("visit")
    local_rows, breadth = template.shape[1:]
    height = local_rows * n_visit
    entries, edge = blocks.shape[2:4]
    places = n_patch * CAP
    scaled = (coeffs[0][:, None] * basis_cols).astype(BF16)
    count = basis_rows.shape[0]
    dma = pltpu.SemaphoreType.DMA
    difference = pl.pallas_call(
        functools.partial(
            exchange_kernel, n_patch, n_visit, (basis_rows.shape[1] // 2, basis_cols.shape[1] // 2)
        ),
        out_shape=jax.ShapeDtypeStruct((height, breadth + LANE), BF16),
        in_specs=[SMEM, SMEM, SMEM, ANY, ANY, VMEM, VMEM],
        out_specs=VMEM,
        scratch_shapes=[
            pltpu.VMEM((entries, edge, edge), BF16),
            pltpu.VMEM((places, edge, edge), BF16),
            pltpu.VMEM((places, edge, edge), BF16),
            pltpu.VMEM((places, 8, LANE), jnp.int32),
            pltpu.VMEM((places, 8, LANE), jnp.int32),
            pltpu.VMEM((height, breadth), BF16),
            pltpu.VMEM((height, breadth), F32),
        ]
        + stencil_scratch(count, height, breadth)
        + [
            dma(()),
            dma(()),
            dma((n_patch - 1,)),
            dma((n_patch,)),
            dma((n_patch - 1,)),
            dma((n_patch,)),
            dma((n_visit - 1,)),
            dma((n_visit,)),
        ],
        compiler_params=pltpu.CompilerParams(
            collective_id=0, has_side_effects=True, vmem_limit_bytes=VMEM_LIMIT
        ),
    )(
        block_patch.reshape(entries), block_slot.reshape(entries), block_count.reshape(1),
        blocks[0, 0], template[0], padded(basis_rows, True), padded(scaled, False),
    )
    psf_count = psf_rows.shape[1]
    filtered = pl.pallas_call(
        functools.partial(filter_kernel, (psf_rows.shape[2] // 2, psf_cols.shape[2] // 2)),
        out_shape=jax.ShapeDtypeStruct((height, breadth), F32),
        grid=(breadth // WIN,),
        in_specs=[
            pl.BlockSpec((height, breadth + LANE), lambda i: (0, 0)),
            pl.BlockSpec((psf_count, WIN), lambda i: (0, 0)),
            pl.BlockSpec((psf_count, WIN), lambda i: (0, 0)),
        ],
        out_specs=pl.BlockSpec((height, WIN), lambda i: (0, i)),
        scratch_shapes=stencil_scratch(psf_count, height, breadth)[1:],
    )(difference, padded(psf_rows[0], True), padded(psf_cols[0], False))
    return filtered[None, None]


def solution(mesh):
    return jax.shard_map(
        per_device,
        mesh=mesh,
        in_specs=(
            P("patch", "visit", None, None, None),
            P("patch", "visit", None, None),
            P("patch", "visit", None),
            P("patch", "visit"),
            P("patch", "visit", None),
            P(),
            P(),
            P("visit", None),
            P("visit", None, None),
            P("visit", None, None),
        ),
        out_specs=P("patch", "visit", None, None),
        check_vma=False,
    )
```

```python
import functools

import jax
import jax.numpy as jnp
from jax import lax
from jax.experimental import pallas as pl
from jax.experimental.pallas import tpu as pltpu
from jax.sharding import PartitionSpec as P

CAP = 2
LANE = 128
HALF = 64
WIN = 256
F32 = jnp.float32
BF16 = jnp.bfloat16
VMEM_LIMIT = 56 * 1024 * 1024


def toeplitz(row, half_len):
    wide = jnp.broadcast_to(row, (LANE, WIN))
    return pltpu.roll(wide, (HALF - half_len) // 8 * 8, 1, stride=1, stride_axis=0)


def spread(taps, staged):
    count, length = taps.shape
    staged[...] = jnp.zeros(staged.shape, F32)
    staged[:count, :length] = taps
    lead = (HALF - length // 2) % 8
    if lead:
        staged[...] = pltpu.roll(staged[...], lead, 1)


def shift_into(load_tile, shifted, height, tiles, step):
    def body(r, carry):
        rows = pl.ds(pl.multiple_of(r * step, step), step)
        lane = lax.broadcasted_iota(jnp.int32, (step, LANE), 1)
        before = jnp.zeros((step, LANE), F32)
        for t in range(tiles):
            rolled = pltpu.roll(load_tile(rows, t), HALF, 1)
            shifted[rows, t * LANE : (t + 1) * LANE] = jnp.where(lane < HALF, before, rolled).astype(BF16)
            before = rolled
        shifted[rows, tiles * LANE :] = jnp.where(lane < HALF, before, 0.0).astype(BF16)
        return carry

    lax.fori_loop(0, height // step, body, 0)


def columns_pass(shifted, tables, smooth, pair, count, height):
    for side in range(2):
        start = pl.multiple_of((2 * pair + side) * LANE, LANE)
        window = shifted[:, pl.ds(start, WIN)]
        for group in range(0, count, 2):
            taken = min(2, count - group)
            got = jnp.dot(
                window, tables[:, group * LANE : (group + taken) * LANE], preferred_element_type=F32
            ).astype(BF16)
            for k in range(taken):
                smooth[group + k, HALF : HALF + height, side * LANE : (side + 1) * LANE] = got[
                    :, k * LANE : (k + 1) * LANE
                ]


def rows_pass(smooth, tables, count, r):
    start = pl.multiple_of(r * LANE, LANE)
    total = jnp.zeros((LANE, WIN), F32)
    for k in range(count):
        total = total + jnp.dot(tables[k], smooth[k, pl.ds(start, WIN), :], preferred_element_type=F32)
    return total


def build_tables(column_taps, row_taps, column_tables, row_tables, staged):
    spread(column_taps, staged)
    for k in range(column_taps.shape[0]):
        table = toeplitz(staged[k : k + 1, :], column_taps.shape[1] // 2)
        column_tables[:, k * LANE : (k + 1) * LANE] = table.T.astype(BF16)
    spread(row_taps, staged)
    for k in range(row_taps.shape[0]):
        row_tables[k] = toeplitz(staged[k : k + 1, :], row_taps.shape[1] // 2).astype(BF16)


def clear_edges(smooth, count, height):
    for k in range(count):
        smooth[k, :HALF, :] = jnp.zeros((HALF, smooth.shape[2]), BF16)
        smooth[k, HALF + height :, :] = jnp.zeros((HALF, smooth.shape[2]), BF16)


def exchange_kernel(
    n_patch, n_visit,
    patch, slot, live, coeffs, blocks, template, basis_rows, basis_cols, psf_rows, psf_cols,
    difference, psf_column_tables, psf_row_tables,
    staged, raw, outgoing, arrived, labels_out, labels_in, whole, total, shifted, column_tables, row_tables, smooth,
    load_sem, own_sem, block_send, block_recv, label_send, label_recv, rows_send, rows_recv,
):
    me = lax.axis_index("patch")
    my_visit = lax.axis_index("visit")
    local_rows, breadth = template.shape
    height = local_rows * n_visit
    entries, edge = blocks.shape[:2]
    count = basis_rows.shape[0]
    wide = breadth // edge
    chips = n_patch // 2
    chip, core = me // 2, lax.rem(me, 2)
    turn = 1 - 2 * (me // chips)
    peers = [2 * chip + 1 - core]
    for hop in range(chips - 1, 0, -1):
        there = 2 * lax.rem(chip + turn * hop + chips, chips)
        peers += [there + core, there + 1 - core]
    visits = [lax.rem(my_visit + hop, n_visit) for hop in range(1, n_visit)]

    load = pltpu.make_async_copy(blocks, raw, load_sem)
    load.start()
    my_rows = pl.ds(pl.multiple_of(my_visit * local_rows, local_rows), local_rows)
    own = pltpu.make_async_copy(template, whole.at[my_rows], own_sem)
    own.start()
    barrier = pltpu.get_barrier_semaphore()
    for peer in peers:
        pl.semaphore_signal(barrier, inc=1, device_id={"patch": peer}, device_id_type=pl.DeviceIdType.MESH)
    for visit in visits:
        pl.semaphore_signal(barrier, inc=1, device_id={"visit": visit}, device_id_type=pl.DeviceIdType.MESH)

    targets = [patch[i] for i in range(entries)]
    place_of = []
    for i in range(entries):
        earlier = jnp.int32(0)
        for before in range(i):
            earlier = earlier + jnp.where(targets[before] == targets[i], 1, 0)
        place_of.append(targets[i] * CAP + earlier)
    marks = [jnp.where(i < live[0, 0], slot[i] + 1, 0) for i in range(entries)]
    load.wait()

    def pack(d, carry):
        source = jnp.int32(0)
        label = jnp.int32(-1)
        for i in range(entries):
            source = source + jnp.where(place_of[i] == d, i, 0)
            label = label + jnp.where(place_of[i] == d, marks[i], 0)
        outgoing[d] = raw[source]
        labels_out[d] = jnp.full((8, LANE), label, jnp.int32)
        return carry

    lax.fori_loop(0, n_patch * CAP, pack, 0)
    pl.semaphore_wait(barrier, n_patch + n_visit - 2)

    row_copies = []
    for hop, visit in enumerate(visits):
        row_copies.append(
            pltpu.make_async_remote_copy(
                src_ref=template, dst_ref=whole.at[my_rows],
                send_sem=rows_send.at[hop], recv_sem=rows_recv.at[my_visit],
                device_id={"visit": visit}, device_id_type=pl.DeviceIdType.MESH,
            )
        )
    copies = []
    for hop, peer in enumerate(peers):
        theirs = pl.ds(peer * CAP, CAP)
        mine = pl.ds(me * CAP, CAP)
        for source, target, send, recv in (
            (labels_out, labels_in, label_send, label_recv),
            (outgoing, arrived, block_send, block_recv),
        ):
            copies.append(
                pltpu.make_async_remote_copy(
                    src_ref=source.at[theirs], dst_ref=target.at[mine],
                    send_sem=send.at[hop], recv_sem=recv.at[me],
                    device_id={"patch": peer}, device_id_type=pl.DeviceIdType.MESH,
                )
            )
    for copy in row_copies:
        copy.start()
    for copy in copies:
        copy.start()

    scaled = jnp.concatenate(
        [(coeffs[0, k] * basis_cols[k : k + 1, :]).astype(BF16).astype(F32) for k in range(count)], axis=0
    )
    build_tables(basis_rows[...].astype(F32), scaled, column_tables, row_tables, staged)
    build_tables(psf_rows[0].astype(F32), psf_cols[0].astype(F32), psf_column_tables, psf_row_tables, staged)
    clear_edges(smooth, count, height)
    own.wait()
    for visit in visits:
        rows = pl.ds(pl.multiple_of(visit * local_rows, local_rows), local_rows)
        pltpu.make_async_copy(whole.at[rows], whole.at[rows], rows_recv.at[visit]).wait()
    shift_into(
        lambda rows, t: whole[rows, t * LANE : (t + 1) * LANE].astype(F32),
        shifted, height, breadth // LANE, 32,
    )

    def per_pair(pair, carry):
        columns_pass(shifted, column_tables, smooth, pair, count, height)

        def per_row(r, inner):
            rows = pl.ds(pl.multiple_of(r * LANE, LANE), LANE)
            columns = pl.ds(pl.multiple_of(pair * WIN, WIN), WIN)
            total[rows, columns] = -rows_pass(smooth, row_tables, count, r)
            return inner

        return lax.fori_loop(0, height // LANE, per_row, carry)

    lax.fori_loop(0, breadth // WIN, per_pair, 0)

    def add_from(held, labels, at):
        step = 16
        marks = [labels[at + c][:1] for c in range(CAP)]
        masks = [[jnp.broadcast_to(jnp.where(mark == s, 1.0, 0.0), (step, LANE)) for mark in marks] for s in range(height // edge * wide)]

        def body(r, carry):
            inside = pl.ds(pl.multiple_of(r * step, step), step)
            for lane in range(0, edge, LANE):
                pieces = [held[at + c, inside, lane : lane + LANE].astype(F32) for c in range(CAP)]
                for s in range(height // edge * wide):
                    rows = pl.ds(pl.multiple_of(s // wide * edge + r * step, step), step)
                    columns = slice(s % wide * edge + lane, s % wide * edge + lane + LANE)
                    value = total[rows, columns]
                    for c in range(CAP):
                        value = value + masks[s][c] * pieces[c]
                    total[rows, columns] = value
            return carry

        lax.fori_loop(0, edge // step, body, 0)

    add_from(outgoing, labels_out, me * CAP)
    for peer in peers:
        theirs = pl.ds(peer * CAP, CAP)
        pltpu.make_async_copy(labels_in.at[theirs], labels_in.at[theirs], label_recv.at[peer]).wait()
        pltpu.make_async_copy(arrived.at[theirs], arrived.at[theirs], block_recv.at[peer]).wait()
        add_from(arrived, labels_in, peer * CAP)
    shift_into(
        lambda rows, t: total[rows, t * LANE : (t + 1) * LANE],
        difference, height, breadth // LANE, 32,
    )
    for copy in row_copies + copies:
        copy.wait_send()


def filter_kernel(difference, column_tables, row_tables, out, smooth):
    height = difference.shape[0]
    count = row_tables.shape[0]
    pair = pl.program_id(0)

    @pl.when(pair == 0)
    def _():
        clear_edges(smooth, count, height)

    columns_pass(difference, column_tables, smooth, pair, count, height)
    for r in range(height // LANE):
        out[r * LANE : (r + 1) * LANE, :] = rows_pass(smooth, row_tables, count, r)


SMEM = pl.BlockSpec(memory_space=pltpu.SMEM)
VMEM = pl.BlockSpec(memory_space=pltpu.VMEM)
ANY = pl.BlockSpec(memory_space=pl.ANY)


def stencil_scratch(count, height, breadth):
    return [
        pltpu.VMEM((height, breadth + LANE), BF16),
        pltpu.VMEM((WIN, count * LANE), BF16),
        pltpu.VMEM((count, LANE, WIN), BF16),
        pltpu.VMEM((count, height + 2 * HALF, WIN), BF16),
    ]


def per_device(blocks, block_patch, block_slot, block_count, template, basis_rows, basis_cols, coeffs, psf_rows, psf_cols):
    n_patch = lax.axis_size("patch")
    n_visit = lax.axis_size("visit")
    local_rows, breadth = template.shape[1:]
    height = local_rows * n_visit
    entries, edge = blocks.shape[2:4]
    places = n_patch * CAP
    count = basis_rows.shape[0]
    psf_count = psf_rows.shape[1]
    dma = pltpu.SemaphoreType.DMA
    difference, psf_column_tables, psf_row_tables = pl.pallas_call(
        functools.partial(
            exchange_kernel, n_patch, n_visit
        ),
        out_shape=(
            jax.ShapeDtypeStruct((height, breadth + LANE), BF16),
            jax.ShapeDtypeStruct((WIN, psf_count * LANE), BF16),
            jax.ShapeDtypeStruct((psf_count, LANE, WIN), BF16),
        ),
        in_specs=[SMEM] * 4 + [ANY] * 2 + [VMEM] * 4,
        out_specs=(VMEM,) * 3,
        scratch_shapes=[
            pltpu.VMEM((pl.cdiv(max(count, psf_count), 8) * 8, WIN), F32),
            pltpu.VMEM((entries, edge, edge), BF16),
            pltpu.VMEM((places, edge, edge), BF16),
            pltpu.VMEM((places, edge, edge), BF16),
            pltpu.VMEM((places, 8, LANE), jnp.int32),
            pltpu.VMEM((places, 8, LANE), jnp.int32),
            pltpu.VMEM((height, breadth), BF16),
            pltpu.VMEM((height, breadth), F32),
        ]
        + stencil_scratch(count, height, breadth)
        + [
            dma(()),
            dma(()),
            dma((n_patch - 1,)),
            dma((n_patch,)),
            dma((n_patch - 1,)),
            dma((n_patch,)),
            dma((n_visit - 1,)),
            dma((n_visit,)),
        ],
        compiler_params=pltpu.CompilerParams(
            collective_id=0, has_side_effects=True, vmem_limit_bytes=VMEM_LIMIT
        ),
    )(
        block_patch.reshape(entries), block_slot.reshape(entries), block_count, coeffs,
        blocks[0, 0], template[0], basis_rows, basis_cols, psf_rows, psf_cols,
    )
    filtered = pl.pallas_call(
        filter_kernel,
        out_shape=jax.ShapeDtypeStruct((height, breadth), F32),
        grid=(breadth // WIN,),
        in_specs=[
            pl.BlockSpec((height, breadth + LANE), lambda i: (0, 0)),
            pl.BlockSpec((WIN, psf_count * LANE), lambda i: (0, 0)),
            pl.BlockSpec((psf_count, LANE, WIN), lambda i: (0, 0, 0)),
        ],
        out_specs=pl.BlockSpec((height, WIN), lambda i: (0, i)),
        scratch_shapes=stencil_scratch(psf_count, height, breadth)[3:],
    )(difference, psf_column_tables, psf_row_tables)
    return filtered[None, None]


def solution(mesh):
    return jax.shard_map(
        per_device,
        mesh=mesh,
        in_specs=(
            P("patch", "visit", None, None, None),
            P("patch", "visit", None, None),
            P("patch", "visit", None),
            P("patch", "visit"),
            P("patch", "visit", None),
            P(),
            P(),
            P("visit", None),
            P("visit", None, None),
            P("visit", None, None),
        ),
        out_specs=P("patch", "visit", None, None),
        check_vma=False,
    )
```

```python
import functools

import jax
import jax.numpy as jnp
from jax import lax
from jax.experimental import pallas as pl
from jax.experimental.pallas import tpu as pltpu
from jax.sharding import PartitionSpec as P

CAP = 2
LANE = 128
HALF = 64
EDGE = 16
WIN = 256
F32 = jnp.float32
BF16 = jnp.bfloat16
VMEM_LIMIT = 32 * 1024 * 1024


def toeplitz(row, half_len):
    wide = jnp.broadcast_to(row, (LANE, WIN))
    return pltpu.roll(wide, (HALF - half_len) // 8 * 8, 1, stride=1, stride_axis=0)


def spread(taps, staged):
    count, length = taps.shape
    staged[...] = jnp.zeros(staged.shape, F32)
    staged[:count, :length] = taps
    lead = (HALF - length // 2) % 8
    if lead:
        staged[...] = pltpu.roll(staged[...], lead, 1)


def shift_into(load_tile, shifted, height, tiles, step):
    def body(r, carry):
        rows = pl.ds(pl.multiple_of(r * step, step), step)
        lane = lax.broadcasted_iota(jnp.int32, (step, LANE), 1)
        before = jnp.zeros((step, LANE), F32)
        for t in range(tiles):
            rolled = pltpu.roll(load_tile(rows, t), HALF, 1)
            shifted[rows, t * LANE : (t + 1) * LANE] = jnp.where(lane < HALF, before, rolled).astype(BF16)
            before = rolled
        shifted[rows, tiles * LANE :] = jnp.where(lane < HALF, before, 0.0).astype(BF16)
        return carry

    lax.fori_loop(0, height // step, body, 0)


def columns_pass(shifted, tables, smooth, pair, count, height, margin=HALF):
    for side in range(2):
        start = pl.multiple_of((2 * pair + side) * LANE, LANE)
        window = shifted[:, pl.ds(start, WIN)]
        for group in range(0, count, 2):
            taken = min(2, count - group)
            got = jnp.dot(
                window, tables[:, group * LANE : (group + taken) * LANE], preferred_element_type=F32
            ).astype(BF16)
            for k in range(taken):
                smooth[group + k, margin : margin + height, side * LANE : (side + 1) * LANE] = got[
                    :, k * LANE : (k + 1) * LANE
                ]


def rows_pass(smooth, tables, count, r):
    start = pl.multiple_of(r * LANE, LANE)
    total = jnp.zeros((LANE, WIN), F32)
    for k in range(count):
        total = total + jnp.dot(tables[k], smooth[k, pl.ds(start, WIN), :], preferred_element_type=F32)
    return total


def band(row, half_len):
    parts = []
    for start in range(0, WIN + 2 * EDGE, EDGE):
        shift = (start - EDGE - half_len - (HALF - half_len) % 8) % WIN
        wide = jnp.broadcast_to(row, (EDGE, WIN))
        rolled = pltpu.roll(wide, shift, 1, stride=1, stride_axis=0)
        offset = (
            lax.broadcasted_iota(jnp.int32, (EDGE, WIN), 1)
            - lax.broadcasted_iota(jnp.int32, (EDGE, WIN), 0) - start + EDGE
        )
        parts.append(jnp.where((offset >= -half_len) & (offset <= half_len), rolled, 0.0))
    return parts


def build_tables(column_taps, row_taps, column_tables, row_tables, staged):
    spread(column_taps, staged)
    for k in range(column_taps.shape[0]):
        table = toeplitz(staged[k : k + 1, :], column_taps.shape[1] // 2)
        column_tables[:, k * LANE : (k + 1) * LANE] = table.T.astype(BF16)
    spread(row_taps, staged)
    for k in range(row_taps.shape[0]):
        half_len = row_taps.shape[1] // 2
        if row_tables.shape[1] == LANE:
            row_tables[k] = toeplitz(staged[k : k + 1, :], half_len).astype(BF16)
        else:
            for part, rows in enumerate(band(staged[k : k + 1, :], half_len)):
                row_tables[k, part * EDGE : (part + 1) * EDGE, :] = rows.astype(BF16)


def clear_edges(smooth, count, height):
    for k in range(count):
        smooth[k, :HALF, :] = jnp.zeros((HALF, smooth.shape[2]), BF16)
        smooth[k, HALF + height :, :] = jnp.zeros((HALF, smooth.shape[2]), BF16)


def exchange_kernel(
    n_patch, n_visit,
    live, patch_in, slot_in, coeffs_in, basis_rows_in, basis_cols_in, psf_rows_in, psf_cols_in, blocks, template,
    difference, psf_column_tables, psf_row_tables,
    patch, slot, coeffs, basis_rows, basis_cols, psf_rows, psf_cols, small_sems, sources, staged, raw, outgoing, arrived, labels_out, labels_in, whole, total, shifted, column_tables, row_tables, smooth,
    load_sem, own_sem, block_send, block_recv, label_send, label_recv, rows_send, rows_recv,
):
    me = lax.axis_index("patch")
    my_visit = lax.axis_index("visit")
    local_rows, breadth = template.shape
    height = local_rows * n_visit
    entries, edge = blocks.shape[:2]
    count = basis_rows.shape[0]
    wide = breadth // edge
    chips = n_patch // 2
    chip, core = me // 2, lax.rem(me, 2)
    turn = 1 - 2 * (me // chips)
    peers = [2 * chip + 1 - core]
    for hop in range(chips - 1, 0, -1):
        there = 2 * lax.rem(chip + turn * hop + chips, chips)
        peers += [there + core, there + 1 - core]
    visits = [lax.rem(my_visit + hop, n_visit) for hop in range(1, n_visit)]

    small = [
        pltpu.make_async_copy(source, held, small_sems.at[i])
        for i, (source, held) in enumerate(
            (
                (patch_in, patch), (slot_in, slot), (coeffs_in, coeffs),
                (basis_rows_in, basis_rows), (basis_cols_in, basis_cols),
                (psf_rows_in, psf_rows), (psf_cols_in, psf_cols),
            )
        )
    ]
    for copy in small:
        copy.start()
    load = pltpu.make_async_copy(blocks, raw, load_sem)
    load.start()
    my_rows = pl.ds(pl.multiple_of(my_visit * local_rows, local_rows), local_rows)
    own = pltpu.make_async_copy(template, whole.at[my_rows], own_sem)
    own.start()
    barrier = pltpu.get_barrier_semaphore()
    for peer in peers:
        pl.semaphore_signal(barrier, inc=1, device_id={"patch": peer}, device_id_type=pl.DeviceIdType.MESH)
    for visit in visits:
        pl.semaphore_signal(barrier, inc=1, device_id={"visit": visit}, device_id_type=pl.DeviceIdType.MESH)

    for copy in small[:2]:
        copy.wait()
    targets = [patch[i] for i in range(entries)]
    place_of = []
    for i in range(entries):
        earlier = jnp.int32(0)
        for before in range(i):
            earlier = earlier + jnp.where(targets[before] == targets[i], 1, 0)
        place_of.append(targets[i] * CAP + earlier)
    marks = [jnp.where(i < live[0, 0], slot[i] + 1, 0) for i in range(entries)]

    def find(d, carry):
        source = jnp.int32(0)
        label = jnp.int32(-1)
        for i in range(entries):
            source = source + jnp.where(place_of[i] == d, i, 0)
            label = label + jnp.where(place_of[i] == d, marks[i], 0)
        sources[d] = source
        labels_out[d] = jnp.full((8, LANE), label, jnp.int32)
        return carry

    lax.fori_loop(0, n_patch * CAP, find, 0)
    load.wait()

    def pack(d, carry):
        outgoing[d] = raw[sources[d]]
        return carry

    lax.fori_loop(0, n_patch * CAP, pack, 0)
    pl.semaphore_wait(barrier, n_patch + n_visit - 2)

    row_copies = []
    for hop, visit in enumerate(visits):
        row_copies.append(
            pltpu.make_async_remote_copy(
                src_ref=template, dst_ref=whole.at[my_rows],
                send_sem=rows_send.at[hop], recv_sem=rows_recv.at[my_visit],
                device_id={"visit": visit}, device_id_type=pl.DeviceIdType.MESH,
            )
        )
    copies = []
    for hop, peer in enumerate(peers):
        theirs = pl.ds(peer * CAP, CAP)
        mine = pl.ds(me * CAP, CAP)
        for source, target, send, recv in (
            (labels_out, labels_in, label_send, label_recv),
            (outgoing, arrived, block_send, block_recv),
        ):
            copies.append(
                pltpu.make_async_remote_copy(
                    src_ref=source.at[theirs], dst_ref=target.at[mine],
                    send_sem=send.at[hop], recv_sem=recv.at[me],
                    device_id={"patch": peer}, device_id_type=pl.DeviceIdType.MESH,
                )
            )
    for copy in row_copies:
        copy.start()
    for copy in copies:
        copy.start()

    for copy in small[2:]:
        copy.wait()
    scaled = jnp.concatenate(
        [(coeffs[0, k] * basis_cols[k : k + 1, :]).astype(BF16).astype(F32) for k in range(count)], axis=0
    )
    build_tables(basis_rows[...].astype(F32), scaled, column_tables, row_tables, staged)
    build_tables(psf_rows[0].astype(F32), psf_cols[0].astype(F32), psf_column_tables, psf_row_tables, staged)
    clear_edges(smooth, count, height)
    own.wait()
    for visit in visits:
        rows = pl.ds(pl.multiple_of(visit * local_rows, local_rows), local_rows)
        pltpu.make_async_copy(whole.at[rows], whole.at[rows], rows_recv.at[visit]).wait()
    shift_into(
        lambda rows, t: whole[rows, t * LANE : (t + 1) * LANE].astype(F32),
        shifted, height, breadth // LANE, 32,
    )

    def per_pair(pair, carry):
        columns_pass(shifted, column_tables, smooth, pair, count, height)

        def per_row(r, inner):
            rows = pl.ds(pl.multiple_of(r * LANE, LANE), LANE)
            columns = pl.ds(pl.multiple_of(pair * WIN, WIN), WIN)
            total[rows, columns] = -rows_pass(smooth, row_tables, count, r)
            return inner

        return lax.fori_loop(0, height // LANE, per_row, carry)

    lax.fori_loop(0, breadth // WIN, per_pair, 0)

    def add_from(held, labels, at):
        step = 16
        marks = [labels[at + c] for c in range(CAP)]
        masks = [[jnp.where(mark == s, 1.0, 0.0) for mark in marks] for s in range(height // edge * wide)]

        def body(r, carry):
            inside = pl.ds(pl.multiple_of(r * step, step), step)
            for lane in range(0, edge, LANE):
                pieces = [
                    held[at + c, inside, lane : lane + LANE].astype(F32).reshape(step // 8, 8, LANE)
                    for c in range(CAP)
                ]
                for s in range(height // edge * wide):
                    rows = pl.ds(pl.multiple_of(s // wide * edge + r * step, step), step)
                    columns = slice(s % wide * edge + lane, s % wide * edge + lane + LANE)
                    value = total[rows, columns].reshape(step // 8, 8, LANE)
                    for c in range(CAP):
                        value = value + masks[s][c][None] * pieces[c]
                    total[rows, columns] = value.reshape(step, LANE)
            return carry

        lax.fori_loop(0, edge // step, body, 0)

    add_from(outgoing, labels_out, me * CAP)
    for peer in peers:
        theirs = pl.ds(peer * CAP, CAP)
        pltpu.make_async_copy(labels_in.at[theirs], labels_in.at[theirs], label_recv.at[peer]).wait()
        pltpu.make_async_copy(arrived.at[theirs], arrived.at[theirs], block_recv.at[peer]).wait()
        add_from(arrived, labels_in, peer * CAP)
    shift_into(
        lambda rows, t: total[rows, t * LANE : (t + 1) * LANE],
        difference, height, breadth // LANE, 32,
    )
    for copy in row_copies + copies:
        copy.wait_send()


def filter_kernel(difference, column_tables, row_tables, out, smooth):
    height = difference.shape[0]
    count = row_tables.shape[0]
    pair = pl.program_id(0)
    columns_pass(difference, column_tables, smooth, pair, count, height, 0)
    chunks = height // WIN
    for chunk in range(chunks):
        first, last = chunk == 0, chunk == chunks - 1
        low = EDGE if first else 0
        high = WIN + EDGE if last else WIN + 2 * EDGE
        got = jnp.zeros((high - low, WIN), F32)
        for k in range(count):
            got = got + jnp.dot(
                row_tables[k, low:high, :], smooth[k, chunk * WIN : (chunk + 1) * WIN, :], preferred_element_type=F32
            )
        start = chunk * WIN - EDGE + low
        if first:
            out[start : start + high - low, :] = got
        else:
            out[start : start + 2 * EDGE, :] = out[start : start + 2 * EDGE, :] + got[: 2 * EDGE]
            out[start + 2 * EDGE : start + high - low, :] = got[2 * EDGE :]


SMEM = pl.BlockSpec(memory_space=pltpu.SMEM)
HBM = pl.BlockSpec(memory_space=pltpu.HBM)
VMEM = pl.BlockSpec(memory_space=pltpu.VMEM)


def stencil_scratch(count, height, breadth):
    return [
        pltpu.VMEM((height, breadth + LANE), BF16),
        pltpu.VMEM((WIN, count * LANE), BF16),
        pltpu.VMEM((count, LANE, WIN), BF16),
        pltpu.VMEM((count, height + 2 * HALF, WIN), BF16),
    ]


def per_device(blocks, block_patch, block_slot, block_count, template, basis_rows, basis_cols, coeffs, psf_rows, psf_cols):
    n_patch = lax.axis_size("patch")
    n_visit = lax.axis_size("visit")
    local_rows, breadth = template.shape[1:]
    height = local_rows * n_visit
    entries, edge = blocks.shape[2:4]
    places = n_patch * CAP
    count = basis_rows.shape[0]
    psf_count = psf_rows.shape[1]
    dma = pltpu.SemaphoreType.DMA
    difference, psf_column_tables, psf_row_tables = pl.pallas_call(
        functools.partial(
            exchange_kernel, n_patch, n_visit
        ),
        out_shape=(
            jax.ShapeDtypeStruct((height, breadth + LANE), BF16),
            jax.ShapeDtypeStruct((WIN, psf_count * LANE), BF16),
            jax.ShapeDtypeStruct((psf_count, WIN + 2 * EDGE, WIN), BF16),
        ),
        in_specs=[SMEM] + [HBM] * 9,
        out_specs=(VMEM,) * 3,
        scratch_shapes=[
            pltpu.SMEM((entries,), jnp.int32),
            pltpu.SMEM((entries,), jnp.int32),
            pltpu.SMEM(coeffs.shape, F32),
            pltpu.VMEM(basis_rows.shape, BF16),
            pltpu.VMEM(basis_cols.shape, F32),
            pltpu.VMEM(psf_rows.shape, BF16),
            pltpu.VMEM(psf_cols.shape, BF16),
            dma((7,)),
            pltpu.SMEM((places,), jnp.int32),
            pltpu.VMEM((pl.cdiv(max(count, psf_count), 8) * 8, WIN), F32),
            pltpu.VMEM((entries, edge, edge), BF16),
            pltpu.VMEM((places, edge, edge), BF16),
            pltpu.VMEM((places, edge, edge), BF16),
            pltpu.VMEM((places, 8, LANE), jnp.int32),
            pltpu.VMEM((places, 8, LANE), jnp.int32),
            pltpu.VMEM((height, breadth), BF16),
            pltpu.VMEM((height, breadth), F32),
        ]
        + stencil_scratch(count, height, breadth)
        + [
            dma(()),
            dma(()),
            dma((n_patch - 1,)),
            dma((n_patch,)),
            dma((n_patch - 1,)),
            dma((n_patch,)),
            dma((n_visit - 1,)),
            dma((n_visit,)),
        ],
        compiler_params=pltpu.CompilerParams(
            collective_id=0, has_side_effects=True, vmem_limit_bytes=VMEM_LIMIT
        ),
    )(
        block_count,
        *(
            pltpu.with_memory_space_constraint(value, pltpu.HBM)
            for value in (
                block_patch.reshape(entries), block_slot.reshape(entries), coeffs,
                basis_rows, basis_cols, psf_rows, psf_cols, blocks[0, 0], template[0],
            )
        )
    )
    filtered = pl.pallas_call(
        filter_kernel,
        out_shape=jax.ShapeDtypeStruct((height, breadth), F32),
        grid=(breadth // WIN,),
        in_specs=[
            pl.BlockSpec((height, breadth + LANE), lambda i: (0, 0)),
            pl.BlockSpec((WIN, psf_count * LANE), lambda i: (0, 0)),
            pl.BlockSpec((psf_count, WIN + 2 * EDGE, WIN), lambda i: (0, 0, 0)),
        ],
        out_specs=pl.BlockSpec((height, WIN), lambda i: (0, i)),
        scratch_shapes=[pltpu.VMEM((psf_count, height, WIN), BF16)],
        compiler_params=pltpu.CompilerParams(vmem_limit_bytes=16 * 1024 * 1024),
    )(difference, psf_column_tables, psf_row_tables)
    return filtered[None, None]


def solution(mesh):
    return jax.shard_map(
        per_device,
        mesh=mesh,
        in_specs=(
            P("patch", "visit", None, None, None),
            P("patch", "visit", None, None),
            P("patch", "visit", None),
            P("patch", "visit"),
            P("patch", "visit", None),
            P(),
            P(),
            P("visit", None),
            P("visit", None, None),
            P("visit", None, None),
        ),
        out_specs=P("patch", "visit", None, None),
        check_vma=False,
    )
```

```python
import functools

import jax
import jax.numpy as jnp
from jax import lax
from jax.experimental import pallas as pl
from jax.experimental.pallas import tpu as pltpu
from jax.sharding import PartitionSpec as P

CAP = 2
LANE = 128
HALF = 64
EDGE = 16
WIN = 256
F32 = jnp.float32
BF16 = jnp.bfloat16
VMEM_LIMIT = 32 * 1024 * 1024


def toeplitz(row, half_len):
    wide = jnp.broadcast_to(row, (LANE, WIN))
    return pltpu.roll(wide, (HALF - half_len) // 8 * 8, 1, stride=1, stride_axis=0)


def spread(taps, staged):
    count, length = taps.shape
    staged[...] = jnp.zeros(staged.shape, F32)
    staged[:count, :length] = taps
    lead = (HALF - length // 2) % 8
    if lead:
        staged[...] = pltpu.roll(staged[...], lead, 1)


def shift_into(load_tile, shifted, height, tiles, step):
    def body(r, carry):
        rows = pl.ds(pl.multiple_of(r * step, step), step)
        lane = lax.broadcasted_iota(jnp.int32, (step, LANE), 1)
        before = jnp.zeros((step, LANE), F32)
        for t in range(tiles):
            rolled = pltpu.roll(load_tile(rows, t), HALF, 1)
            shifted[rows, t * LANE : (t + 1) * LANE] = jnp.where(lane < HALF, before, rolled).astype(BF16)
            before = rolled
        shifted[rows, tiles * LANE :] = jnp.where(lane < HALF, before, 0.0).astype(BF16)
        return carry

    lax.fori_loop(0, height // step, body, 0)


def columns_pass(shifted, tables, smooth, pair, count, height, margin=HALF):
    for side in range(2):
        start = pl.multiple_of((2 * pair + side) * LANE, LANE)
        window = shifted[:, pl.ds(start, WIN)]
        for group in range(0, count, 2):
            taken = min(2, count - group)
            got = jnp.dot(
                window, tables[:, group * LANE : (group + taken) * LANE], preferred_element_type=F32
            ).astype(BF16)
            for k in range(taken):
                smooth[group + k, margin : margin + height, side * LANE : (side + 1) * LANE] = got[
                    :, k * LANE : (k + 1) * LANE
                ]


def rows_pass(smooth, tables, count, r):
    start = pl.multiple_of(r * LANE, LANE)
    total = jnp.zeros((LANE, WIN), F32)
    for k in range(count):
        total = total + jnp.dot(tables[k], smooth[k, pl.ds(start, WIN), :], preferred_element_type=F32)
    return total


def band(row, half_len):
    parts = []
    for start in range(0, WIN + 2 * EDGE, EDGE):
        shift = (start - EDGE - half_len - (HALF - half_len) % 8) % WIN
        wide = jnp.broadcast_to(row, (EDGE, WIN))
        rolled = pltpu.roll(wide, shift, 1, stride=1, stride_axis=0)
        offset = (
            lax.broadcasted_iota(jnp.int32, (EDGE, WIN), 1)
            - lax.broadcasted_iota(jnp.int32, (EDGE, WIN), 0) - start + EDGE
        )
        parts.append(jnp.where((offset >= -half_len) & (offset <= half_len), rolled, 0.0))
    return parts


def build_tables(column_taps, row_taps, column_tables, row_tables, staged):
    spread(column_taps, staged)
    for k in range(column_taps.shape[0]):
        table = toeplitz(staged[k : k + 1, :], column_taps.shape[1] // 2)
        column_tables[:, k * LANE : (k + 1) * LANE] = table.T.astype(BF16)
    spread(row_taps, staged)
    for k in range(row_taps.shape[0]):
        half_len = row_taps.shape[1] // 2
        if row_tables.shape[1] == LANE:
            row_tables[k] = toeplitz(staged[k : k + 1, :], half_len).astype(BF16)
        else:
            for part, rows in enumerate(band(staged[k : k + 1, :], half_len)):
                row_tables[k, part * EDGE : (part + 1) * EDGE, :] = rows.astype(BF16)


def clear_edges(smooth, count, height):
    for k in range(count):
        smooth[k, :HALF, :] = jnp.zeros((HALF, smooth.shape[2]), BF16)
        smooth[k, HALF + height :, :] = jnp.zeros((HALF, smooth.shape[2]), BF16)


def exchange_kernel(
    n_patch, n_visit,
    live, patch_in, slot_in, coeffs_in, basis_rows_in, basis_cols_in, psf_rows_in, psf_cols_in, blocks, template,
    difference, psf_column_tables, psf_row_tables,
    patch, slot, coeffs, basis_rows, basis_cols, psf_rows, psf_cols, small_sems, sources, staged, raw, outgoing, arrived, labels_out, labels_in, whole, total, shifted, column_tables, row_tables, smooth,
    load_sem, own_sem, block_send, block_recv, label_send, label_recv, rows_send, rows_recv,
):
    me = lax.axis_index("patch")
    my_visit = lax.axis_index("visit")
    local_rows, breadth = template.shape
    height = local_rows * n_visit
    entries, edge = blocks.shape[:2]
    count = basis_rows.shape[0]
    wide = breadth // edge
    chips = n_patch // 2
    chip, core = me // 2, lax.rem(me, 2)
    turn = 1 - 2 * (me // chips)
    peers = [2 * chip + 1 - core]
    for hop in range(chips - 1, 0, -1):
        there = 2 * lax.rem(chip + turn * hop + chips, chips)
        peers += [there + core, there + 1 - core]
    visits = [lax.rem(my_visit + hop, n_visit) for hop in range(1, n_visit)]

    small = [
        pltpu.make_async_copy(source, held, small_sems.at[i])
        for i, (source, held) in enumerate(
            (
                (patch_in, patch), (slot_in, slot), (coeffs_in, coeffs),
                (basis_rows_in, basis_rows), (basis_cols_in, basis_cols),
                (psf_rows_in, psf_rows), (psf_cols_in, psf_cols),
            )
        )
    ]
    for copy in small:
        copy.start()
    load = pltpu.make_async_copy(blocks, raw, load_sem)
    load.start()
    my_rows = pl.ds(pl.multiple_of(my_visit * local_rows, local_rows), local_rows)
    own = pltpu.make_async_copy(template, whole.at[my_rows], own_sem)
    own.start()
    barrier = pltpu.get_barrier_semaphore()
    for peer in peers:
        pl.semaphore_signal(barrier, inc=1, device_id={"patch": peer}, device_id_type=pl.DeviceIdType.MESH)
    for visit in visits:
        pl.semaphore_signal(barrier, inc=1, device_id={"visit": visit}, device_id_type=pl.DeviceIdType.MESH)

    for copy in small[:2]:
        copy.wait()
    targets = [patch[i] for i in range(entries)]
    place_of = []
    for i in range(entries):
        earlier = jnp.int32(0)
        for before in range(i):
            earlier = earlier + jnp.where(targets[before] == targets[i], 1, 0)
        place_of.append(targets[i] * CAP + earlier)
    marks = [jnp.where(i < live[0, 0], slot[i] + 1, 0) for i in range(entries)]

    def find(d, carry):
        for c in range(CAP):
            source = jnp.int32(0)
            label = jnp.int32(-1)
            for i in range(entries):
                source = source + jnp.where(place_of[i] == d * CAP + c, i, 0)
                label = label + jnp.where(place_of[i] == d * CAP + c, marks[i], 0)
            sources[d * CAP + c] = source
            labels_out[d, c : c + 1, :] = jnp.full((1, LANE), label, jnp.int32)
        return carry

    lax.fori_loop(0, n_patch, find, 0)
    load.wait()

    def pack(d, carry):
        outgoing[d] = raw[sources[d]]
        return carry

    lax.fori_loop(0, n_patch * CAP, pack, 0)
    pl.semaphore_wait(barrier, n_patch + n_visit - 2)

    row_copies = []
    for hop, visit in enumerate(visits):
        row_copies.append(
            pltpu.make_async_remote_copy(
                src_ref=template, dst_ref=whole.at[my_rows],
                send_sem=rows_send.at[hop], recv_sem=rows_recv.at[my_visit],
                device_id={"visit": visit}, device_id_type=pl.DeviceIdType.MESH,
            )
        )
    copies = []
    for hop, peer in enumerate(peers):
        theirs = pl.ds(peer * CAP, CAP)
        mine = pl.ds(me * CAP, CAP)
        for source, target, send, recv in (
            (labels_out.at[peer], labels_in.at[me], label_send, label_recv),
            (outgoing.at[theirs], arrived.at[mine], block_send, block_recv),
        ):
            copies.append(
                pltpu.make_async_remote_copy(
                    src_ref=source, dst_ref=target,
                    send_sem=send.at[hop], recv_sem=recv.at[me],
                    device_id={"patch": peer}, device_id_type=pl.DeviceIdType.MESH,
                )
            )
    for copy in row_copies:
        copy.start()
    for copy in copies:
        copy.start()

    for copy in small[2:]:
        copy.wait()
    scaled = jnp.concatenate(
        [(coeffs[0, k] * basis_cols[k : k + 1, :]).astype(BF16).astype(F32) for k in range(count)], axis=0
    )
    build_tables(basis_rows[...].astype(F32), scaled, column_tables, row_tables, staged)
    build_tables(psf_rows[0].astype(F32), psf_cols[0].astype(F32), psf_column_tables, psf_row_tables, staged)
    clear_edges(smooth, count, height)
    own.wait()
    for visit in visits:
        rows = pl.ds(pl.multiple_of(visit * local_rows, local_rows), local_rows)
        pltpu.make_async_copy(whole.at[rows], whole.at[rows], rows_recv.at[visit]).wait()
    shift_into(
        lambda rows, t: whole[rows, t * LANE : (t + 1) * LANE].astype(F32),
        shifted, height, breadth // LANE, 32,
    )

    def per_pair(pair, carry):
        columns_pass(shifted, column_tables, smooth, pair, count, height)

        def per_row(r, inner):
            rows = pl.ds(pl.multiple_of(r * LANE, LANE), LANE)
            columns = pl.ds(pl.multiple_of(pair * WIN, WIN), WIN)
            total[rows, columns] = -rows_pass(smooth, row_tables, count, r)
            return inner

        return lax.fori_loop(0, height // LANE, per_row, carry)

    lax.fori_loop(0, breadth // WIN, per_pair, 0)

    def add_from(held, labels, source):
        step = 16
        at = source * CAP
        marks = [labels[source, c : c + 1, :] for c in range(CAP)]
        masks = [[jnp.broadcast_to(jnp.where(mark == s, 1.0, 0.0), (8, LANE)) for mark in marks] for s in range(height // edge * wide)]

        def body(r, carry):
            inside = pl.ds(pl.multiple_of(r * step, step), step)
            for lane in range(0, edge, LANE):
                pieces = [
                    held[at + c, inside, lane : lane + LANE].astype(F32).reshape(step // 8, 8, LANE)
                    for c in range(CAP)
                ]
                for s in range(height // edge * wide):
                    rows = pl.ds(pl.multiple_of(s // wide * edge + r * step, step), step)
                    columns = slice(s % wide * edge + lane, s % wide * edge + lane + LANE)
                    value = total[rows, columns].reshape(step // 8, 8, LANE)
                    for c in range(CAP):
                        value = value + masks[s][c][None] * pieces[c]
                    total[rows, columns] = value.reshape(step, LANE)
            return carry

        lax.fori_loop(0, edge // step, body, 0)

    add_from(outgoing, labels_out, me)
    for peer in peers:
        theirs = pl.ds(peer * CAP, CAP)
        pltpu.make_async_copy(labels_in.at[peer], labels_in.at[peer], label_recv.at[peer]).wait()
        pltpu.make_async_copy(arrived.at[theirs], arrived.at[theirs], block_recv.at[peer]).wait()
        add_from(arrived, labels_in, peer)
    shift_into(
        lambda rows, t: total[rows, t * LANE : (t + 1) * LANE],
        difference, height, breadth // LANE, 32,
    )
    for copy in row_copies + copies:
        copy.wait_send()


def filter_kernel(difference, column_tables, row_tables, out, smooth):
    height = difference.shape[0]
    count = row_tables.shape[0]
    pair = pl.program_id(0)
    columns_pass(difference, column_tables, smooth, pair, count, height, 0)
    chunks = height // WIN
    for chunk in range(chunks):
        first, last = chunk == 0, chunk == chunks - 1
        low = EDGE if first else 0
        high = WIN + EDGE if last else WIN + 2 * EDGE
        got = jnp.zeros((high - low, WIN), F32)
        for k in range(count):
            got = got + jnp.dot(
                row_tables[k, low:high, :], smooth[k, chunk * WIN : (chunk + 1) * WIN, :], preferred_element_type=F32
            )
        start = chunk * WIN - EDGE + low
        if first:
            out[start : start + high - low, :] = got
        else:
            out[start : start + 2 * EDGE, :] = out[start : start + 2 * EDGE, :] + got[: 2 * EDGE]
            out[start + 2 * EDGE : start + high - low, :] = got[2 * EDGE :]


SMEM = pl.BlockSpec(memory_space=pltpu.SMEM)
HBM = pl.BlockSpec(memory_space=pltpu.HBM)
VMEM = pl.BlockSpec(memory_space=pltpu.VMEM)


def stencil_scratch(count, height, breadth):
    return [
        pltpu.VMEM((height, breadth + LANE), BF16),
        pltpu.VMEM((WIN, count * LANE), BF16),
        pltpu.VMEM((count, LANE, WIN), BF16),
        pltpu.VMEM((count, height + 2 * HALF, WIN), BF16),
    ]


def per_device(blocks, block_patch, block_slot, block_count, template, basis_rows, basis_cols, coeffs, psf_rows, psf_cols):
    n_patch = lax.axis_size("patch")
    n_visit = lax.axis_size("visit")
    local_rows, breadth = template.shape[1:]
    height = local_rows * n_visit
    entries, edge = blocks.shape[2:4]
    places = n_patch * CAP
    count = basis_rows.shape[0]
    psf_count = psf_rows.shape[1]
    dma = pltpu.SemaphoreType.DMA
    difference, psf_column_tables, psf_row_tables = pl.pallas_call(
        functools.partial(
            exchange_kernel, n_patch, n_visit
        ),
        out_shape=(
            jax.ShapeDtypeStruct((height, breadth + LANE), BF16),
            jax.ShapeDtypeStruct((WIN, psf_count * LANE), BF16),
            jax.ShapeDtypeStruct((psf_count, WIN + 2 * EDGE, WIN), BF16),
        ),
        in_specs=[SMEM] + [HBM] * 9,
        out_specs=(VMEM,) * 3,
        scratch_shapes=[
            pltpu.SMEM((entries,), jnp.int32),
            pltpu.SMEM((entries,), jnp.int32),
            pltpu.SMEM(coeffs.shape, F32),
            pltpu.VMEM(basis_rows.shape, BF16),
            pltpu.VMEM(basis_cols.shape, F32),
            pltpu.VMEM(psf_rows.shape, BF16),
            pltpu.VMEM(psf_cols.shape, BF16),
            dma((7,)),
            pltpu.SMEM((places,), jnp.int32),
            pltpu.VMEM((pl.cdiv(max(count, psf_count), 8) * 8, WIN), F32),
            pltpu.VMEM((entries, edge, edge), BF16),
            pltpu.VMEM((places, edge, edge), BF16),
            pltpu.VMEM((places, edge, edge), BF16),
            pltpu.VMEM((n_patch, CAP, LANE), jnp.int32),
            pltpu.VMEM((n_patch, CAP, LANE), jnp.int32),
            pltpu.VMEM((height, breadth), BF16),
            pltpu.VMEM((height, breadth), F32),
        ]
        + stencil_scratch(count, height, breadth)
        + [
            dma(()),
            dma(()),
            dma((n_patch - 1,)),
            dma((n_patch,)),
            dma((n_patch - 1,)),
            dma((n_patch,)),
            dma((n_visit - 1,)),
            dma((n_visit,)),
        ],
        compiler_params=pltpu.CompilerParams(
            collective_id=0, has_side_effects=True, vmem_limit_bytes=VMEM_LIMIT
        ),
    )(
        block_count,
        *(
            pltpu.with_memory_space_constraint(value, pltpu.HBM)
            for value in (
                block_patch.reshape(entries), block_slot.reshape(entries), coeffs,
                basis_rows, basis_cols, psf_rows, psf_cols, blocks[0, 0], template[0],
            )
        )
    )
    filtered = pl.pallas_call(
        filter_kernel,
        out_shape=jax.ShapeDtypeStruct((height, breadth), F32),
        grid=(breadth // WIN,),
        in_specs=[
            pl.BlockSpec((height, breadth + LANE), lambda i: (0, 0)),
            pl.BlockSpec((WIN, psf_count * LANE), lambda i: (0, 0)),
            pl.BlockSpec((psf_count, WIN + 2 * EDGE, WIN), lambda i: (0, 0, 0)),
        ],
        out_specs=pl.BlockSpec((height, WIN), lambda i: (0, i)),
        scratch_shapes=[pltpu.VMEM((psf_count, height, WIN), BF16)],
        compiler_params=pltpu.CompilerParams(vmem_limit_bytes=16 * 1024 * 1024),
    )(difference, psf_column_tables, psf_row_tables)
    return filtered[None, None]


def solution(mesh):
    return jax.shard_map(
        per_device,
        mesh=mesh,
        in_specs=(
            P("patch", "visit", None, None, None),
            P("patch", "visit", None, None),
            P("patch", "visit", None),
            P("patch", "visit"),
            P("patch", "visit", None),
            P(),
            P(),
            P("visit", None),
            P("visit", None, None),
            P("visit", None, None),
        ),
        out_specs=P("patch", "visit", None, None),
        check_vma=False,
    )
```
